32 devices in a mesh: pipe: 2 (over y), ctx: 16 (over z, x, core).
Axes of the slice: x: 2, y: 2, z: 4, core: 2. Of those that a mesh axis runs over, the one named last changes fastest.
Arguments:
- saved_qkv: bfloat16 [2, 3, 2048, 2048], P('pipe', None, 'ctx'), may hold values from -6 to 6
- handed: bfloat16 [2, 2048, 2048], P('pipe', 'ctx'), may hold values from -6 to 6
- long_filter: bfloat16 [2, 128, 128], P('pipe'), may hold values from -0.5 to 0.5
- short_filter: bfloat16 [2, 3, 3, 2048], P('pipe'), may hold values from -3.5 to 3.5
- doc_lengths: int32 [16], replicated, may hold values from 1 to 512, 2048 in all
Outputs:
- grad_pre: bfloat16 [2, 3, 2048, 2048], P('pipe', None, 'ctx')
- filter_grad: float32 [2, 128, 128], P('pipe')
The draws below stay inside these ranges and needn't reach their ends.
Inputs may be any that keep to these rules, and one draw needn't show every extreme that they name: `doc_lengths`: documents lie end to end and sum to 2048 tokens; the longest has exactly 512 tokens.
All inputs are finite; a program needn't handle non-finite values.
Results may differ from the reference program's by a relative error of at most 0.0058.
Values may be sent and summed in bfloat16 or wider, within the bound.
A program may use at most 64 MiB of HBM per device.

```python
import math
import jax
import jax.numpy as jnp
import numpy as np
from jax import lax

C = 2048
GCH = 16
TAPS = 128
SHORT = 3
L_DEV = 128
GROUPS = 128
SEQ = 2048
SECTIONS = 2
NDOCS = 16


def block_levels(stream_key, shape, shards, least, top_value):
    level = 1.0
    for axis_at, shards_of in shards:
        draws = jax.random.uniform(jax.random.fold_in(jax.random.fold_in(stream_key, 6), axis_at), (shards_of,), jnp.float32, least / len(shards), top_value / len(shards))
        level = level * jnp.repeat(jnp.exp(draws), shape[axis_at] // shards_of).reshape((-1,) + (1,) * (len(shape) - 1 - axis_at))
    return level


def split_up(count, total, limit, lean):
    portions = [(1 << 20) // math.isqrt(rank ** lean) + 1 for rank in range(2, count + 1)]
    spare, counts = total - limit - (count - 1), [1] * (count - 1)
    while spare > 0:
        movable = [i for i in range(count - 1) if counts[i] < limit]
        pool, left = sum([portions[i] for i in movable]), spare
        for i in movable:
            addition = min(limit - counts[i], max(1, left * portions[i] // pool), spare)
            counts[i] = counts[i] + addition
            spare = spare - addition
    return np.array([limit] + counts)


def ragged(stream_key, count, total, reach, lean):
    if count == 2:
        one = jax.random.randint(stream_key, (), max(1, total - reach), min(reach, total - 1) + 1)
        return jnp.stack([one, total - one])
    tallies = jnp.asarray(split_up(count, total, reach, lean), jnp.int32)
    twos = (count - 1) // 2
    source_of, taker = tallies[1:1 + 2 * twos:2], tallies[2:2 + 2 * twos:2]
    margin = jnp.minimum(source_of - 1, reach - taker)
    moved = jax.random.randint(jax.random.fold_in(stream_key, 1), (twos,), 0, 1 << 20) % (margin + 1)
    tallies = tallies.at[1:1 + 2 * twos:2].set(source_of - moved).at[2:2 + 2 * twos:2].set(taker + moved)
    return tallies[jax.random.permutation(jax.random.fold_in(stream_key, 2), count)]


def bell_draw(own_key, extent, spread, reach, cuts=(), kind=jnp.bfloat16):
    loudness = block_levels(own_key, extent, cuts, -0.22, 0.18) if cuts else 1.0
    result = jax.random.normal(own_key, extent, jnp.float32) * spread * loudness
    return jnp.minimum(jnp.maximum(result, -reach), reach).astype(kind)


def setup_inputs(seed: int = 0) -> dict:
    streams_of = jax.random.split(jax.random.key(seed), 6)
    return {
        "saved_qkv": bell_draw(streams_of[0], (SECTIONS, 3, SEQ, C), 1.0, 6.0, ((0, 2), (2, 16))),
        "handed": bell_draw(streams_of[1], (SECTIONS, SEQ, C), 1.0, 6.0, ((0, 2), (1, 16))),
        "long_filter": bell_draw(streams_of[2], (SECTIONS, TAPS, GROUPS), TAPS ** -0.5, 0.5, ((0, 2),)),
        "short_filter": bell_draw(streams_of[3], (SECTIONS, 3, SHORT, C), SHORT ** -0.5, 3.5, ((0, 2),)),
        "doc_lengths": ragged(streams_of[4], NDOCS, SEQ, 4 * L_DEV, 2).astype(jnp.int32),
    }


def doc_positions(doc_lengths):
    starts = (jnp.cumsum(doc_lengths) - doc_lengths).astype(jnp.int32)
    global_rows = jnp.arange(SEQ, dtype=jnp.int32)
    latest = lax.optimization_barrier(jnp.max(jnp.where(starts[None, :] <= global_rows[:, None], starts[None, :], 0), axis=1))
    return (global_rows - latest).astype(jnp.int32)

def one_section(position, section_args):
    saved_rows, incoming, filt, short_taps = section_args
    query_rows = saved_rows[0].astype(jnp.float32)
    key_rows = saved_rows[1].astype(jnp.float32)
    value_rows = saved_rows[2].astype(jnp.float32)
    product = (key_rows * value_rows).astype(jnp.bfloat16).astype(jnp.float32)
    filt_wide = filt.astype(jnp.float32)
    padded_product = jnp.concatenate([jnp.zeros((TAPS, C), jnp.float32), product], axis=0)
    tap_index = jnp.arange(TAPS, dtype=jnp.int32)

    def forward_step(total, lag):
        shifted = lax.dynamic_slice_in_dim(padded_product, (TAPS - lag).astype(jnp.int32), SEQ, 0)
        weights = jnp.repeat(filt_wide[lag], GCH)
        usable = (lag <= position)[:, None]
        return (total + jnp.where(usable, shifted * weights[None, :], 0.0), None)
    conv_out, _ = lax.scan(forward_step, jnp.zeros((SEQ, C), jnp.float32), tap_index)
    incoming_wide = incoming.astype(jnp.float32)
    conv_grad = (incoming_wide * query_rows).astype(jnp.bfloat16).astype(jnp.float32)
    query_grad = (incoming_wide * conv_out).astype(jnp.bfloat16)
    padded_grad = jnp.concatenate([conv_grad, jnp.zeros((TAPS, C), jnp.float32)], axis=0)
    padded_pos = jnp.concatenate([position, jnp.full((TAPS,), -1, jnp.int32)])

    def backward_step(total, lag):
        ahead = lax.dynamic_slice_in_dim(padded_grad, lag, SEQ, 0)
        ahead_pos = lax.dynamic_slice_in_dim(padded_pos, lag, SEQ, 0)
        weights = jnp.repeat(filt_wide[lag], GCH)
        total = total + jnp.where((lag <= ahead_pos)[:, None], ahead * weights[None, :], 0.0)
        behind = lax.dynamic_slice_in_dim(padded_product, (TAPS - lag).astype(jnp.int32), SEQ, 0)
        pair = lax.optimization_barrier(jnp.sum((conv_grad * behind).reshape(SEQ, GROUPS, GCH), axis=2)).astype(jnp.bfloat16)
        pair = lax.optimization_barrier(pair).astype(jnp.float32)
        column = lax.optimization_barrier(jnp.sum(jnp.where((lag <= position)[:, None], pair, 0.0), axis=0))
        return (total, column)
    mixed_grad, filter_terms = lax.scan(backward_step, jnp.zeros((SEQ, C), jnp.float32), tap_index)
    key_grad = (mixed_grad * value_rows).astype(jnp.bfloat16)
    value_grad = (mixed_grad * key_rows).astype(jnp.bfloat16)
    stacked = jnp.stack([query_grad, key_grad, value_grad]).astype(jnp.float32)
    padded_stack = jnp.concatenate([stacked, jnp.zeros((3, SHORT - 1, C), jnp.float32)], axis=1)
    short_pos = jnp.concatenate([position, jnp.full((SHORT - 1,), -1, jnp.int32)])
    total = jnp.zeros((3, SEQ, C), jnp.float32)
    for shift_by in range(SHORT):
        usable = (shift_by <= short_pos[shift_by:shift_by + SEQ])[None, :, None]
        weights = short_taps[:, shift_by].astype(jnp.float32)[:, None, :]
        total = total + jnp.where(usable, weights * padded_stack[:, shift_by:shift_by + SEQ], 0.0)
    return (total.astype(jnp.bfloat16), filter_terms / math.sqrt(SEQ * GCH))

def reference(saved_qkv, handed, long_filter, short_filter, doc_lengths):
    position = doc_positions(doc_lengths)
    incoming_all = jnp.roll(handed, -1, axis=0)
    grad_pre, filter_grad = lax.map(lambda section_args: one_section(position, section_args), (saved_qkv, incoming_all, long_filter, short_filter))
    return (grad_pre, filter_grad)
```

```python
import functools
import math

import jax
import jax.numpy as jnp
from jax import lax
from jax.experimental import pallas as pl
from jax.experimental.pallas import tpu as pltpu
from jax.sharding import PartitionSpec as P

MESH = pl.DeviceIdType.MESH
F32 = jnp.float32
BF16 = jnp.bfloat16
LANES = 128
RIM = 8
STRIP = 16


def positions(rows, docs_ref):
    latest = jnp.zeros(rows.shape, jnp.int32)
    start = jnp.int32(0)
    for doc in range(docs_ref.shape[0]):
        latest = jnp.maximum(latest, jnp.where(start <= rows, start, 0))
        start = start + docs_ref[doc]
    return rows - latest


def kernel(
    sections, devices, chunks, owners,
    docs_ref, qkv_hbm, handed_hbm, filt_hbm, short_hbm,
    out_hbm, sum_hbm,
    qkv, inc, zz, gg, gback, ysc, dsc, obuf, lhs_f, lhs_b, lhs_p, fdir, frev, filt, short_in, shortf,
    m_own, m_prev, t_own, t_next, r_own, r_prev, u_rows, lane_mask,
    acc, part, parts_in, gath, fg,
    in_sem, par_sem, out_sem, sum_sem, inc_s, inc_r, z_s, z_r, g_s, g_r, rim_s, rim_r, rs_s, rs_r, ag_s, ag_r,
    ready,
):
    sec = lax.axis_index("pipe")
    me = lax.axis_index("ctx")
    count, channels = inc.shape
    groups = fdir.shape[0]
    members = channels // groups
    per_tile = LANES // members
    wide = channels // chunks
    tiles = wide // LANES
    share = groups // owners
    low = (devices - owners) // 2
    first, last = me == 0, me == devices - 1
    ahead = lax.rem(sec + sections - 1, sections)
    behind = lax.rem(sec + 1, sections)
    before, after = jnp.logical_not(first), jnp.logical_not(last)

    barrier = pltpu.get_barrier_semaphore()
    pl.semaphore_signal(barrier, inc=1, device_id={"pipe": behind}, device_id_type=MESH)

    @pl.when(before)
    def _():
        pl.semaphore_signal(barrier, inc=1, device_id={"ctx": me - 1}, device_id_type=MESH)

    @pl.when(after)
    def _():
        pl.semaphore_signal(barrier, inc=1, device_id={"ctx": me + 1}, device_id_type=MESH)

    loads = [
        pltpu.make_async_copy(qkv_hbm.at[0, i], qkv.at[i], in_sem.at[i]) for i in range(3)
    ]
    for i in (1, 2, 0):
        loads[i].start()
    params = [
        pltpu.make_async_copy(filt_hbm.at[0], filt, par_sem.at[0]),
        pltpu.make_async_copy(short_hbm.at[0], short_in, par_sem.at[1]),
    ]
    for copy in params:
        copy.start()

    pl.semaphore_wait(barrier, 1 + before.astype(jnp.int32) + after.astype(jnp.int32))

    reaches = []
    while 2 ** len(reaches) < devices:
        reaches.append(2 ** len(reaches))

    def tell(r):
        if r < len(reaches):
            @pl.when(me >= reaches[r])
            def _():
                pl.semaphore_signal(
                    ready.at[r], inc=1, device_id={"ctx": me - reaches[r]}, device_id_type=MESH)

            @pl.when(me + reaches[r] < devices)
            def _():
                pl.semaphore_signal(
                    ready.at[r], inc=1, device_id={"ctx": me + reaches[r]}, device_id_type=MESH)

    def hear(r):
        if r < len(reaches):
            pl.semaphore_wait(
                ready.at[r],
                (me >= reaches[r]).astype(jnp.int32)
                + (me + reaches[r] < devices).astype(jnp.int32))

    def cols(c):
        return pl.ds(c * wide, wide)

    def send_inc(c):
        return pltpu.make_async_remote_copy(
            handed_hbm.at[0, :, cols(c)], inc.at[:, cols(c)], inc_s.at[c], inc_r.at[c],
            device_id={"pipe": ahead}, device_id_type=MESH)

    def send_z(c):
        return pltpu.make_async_remote_copy(
            zz.at[pl.ds(0, count), cols(c)], zz.at[pl.ds(count, count), cols(c)],
            z_s.at[c], z_r.at[c],
            device_id={"ctx": lax.rem(me + 1, devices)}, device_id_type=MESH)

    def send_g(c):
        return pltpu.make_async_remote_copy(
            gg.at[pl.ds(0, count), cols(c)], gg.at[pl.ds(count, count), cols(c)],
            g_s.at[c], g_r.at[c],
            device_id={"ctx": lax.rem(me + devices - 1, devices)}, device_id_type=MESH)

    def send_rim(c):
        return pltpu.make_async_remote_copy(
            dsc.at[:, pl.ds(0, RIM), cols(c)], dsc.at[:, pl.ds(count, RIM), cols(c)],
            rim_s.at[c], rim_r.at[c],
            device_id={"ctx": lax.rem(me + devices - 1, devices)}, device_id_type=MESH)

    def send_part(o):
        return pltpu.make_async_remote_copy(
            part.at[o], parts_in.at[me], rs_s.at[o], rs_r.at[me],
            device_id={"ctx": low + o}, device_id_type=MESH)

    def take_part(peer):
        return pltpu.make_async_remote_copy(
            part.at[0], parts_in.at[peer], rs_s.at[0], rs_r.at[peer],
            device_id={"ctx": peer}, device_id_type=MESH)

    def send_sum(k):
        return pltpu.make_async_remote_copy(
            gath.at[me - low], gath.at[me - low], ag_s.at[k], ag_r.at[me - low],
            device_id={"ctx": lax.rem(me + k, devices)}, device_id_type=MESH)

    def take_sum(o):
        return pltpu.make_async_remote_copy(
            gath.at[o], gath.at[o], ag_s.at[0], ag_r.at[o],
            device_id={"ctx": low + o}, device_id_type=MESH)

    for c in range(chunks):
        send_inc(c).start()
    tell(0)

    loads[1].wait()
    loads[2].wait()
    for c in range(chunks):
        z = qkv[1, :, cols(c)].astype(F32) * qkv[2, :, cols(c)].astype(F32)
        zz[pl.ds(0, count), cols(c)] = z.astype(BF16)

        @pl.when(after)
        def _():
            send_z(c).start()

    @pl.when(first)
    def _():
        zz[pl.ds(count, count), :] = jnp.zeros((count, channels), BF16)

    @pl.when(last)
    def _():
        gg[pl.ds(count, count), :] = jnp.zeros((count, channels), BF16)
        dsc[:, pl.ds(count, RIM), :] = jnp.zeros((3, RIM, channels), F32)

    square = (count, count)
    down = lax.broadcasted_iota(jnp.int32, square, 0)
    across = lax.broadcasted_iota(jnp.int32, square, 1)
    base = me * count

    def one(flag):
        return jnp.where(flag, 1.0, 0.0).astype(F32)

    pos_down = positions(base + down[:, :LANES], docs_ref)
    lag = down - across
    m_own[...] = one((lag >= 0) & (lag <= pos_down)).astype(BF16)
    m_prev[...] = one((lag < 0) & (lag + count <= pos_down)).astype(BF16)
    turned = count - 1 - down
    pos_turned = positions(base + turned, docs_ref)
    lag = turned - across
    r_own[...] = one((lag >= 0) & (lag <= pos_turned))
    r_prev[...] = one((lag < 0) & (lag + count <= pos_turned))
    line = lax.broadcasted_iota(jnp.int32, (8, count), 1)
    pos_line = positions(base + line, docs_ref)[0:1]
    pos_ahead = positions(base + count + line, docs_ref)[0:1]
    lag = across - down
    t_own[...] = one((lag >= 0) & (lag <= pos_line)).astype(BF16)
    more = jnp.where(last, 0, 1)
    t_next[...] = one((lag < 0) & (lag + count <= pos_ahead) & (more > 0)).astype(BF16)
    for j in range(1, u_rows.shape[0] + 1):
        rows = base + down[:, :LANES] + j
        u_rows[j - 1] = one((j <= positions(rows, docs_ref)) & (rows < devices * count))
    lane_group = lax.broadcasted_iota(jnp.int32, (count, LANES), 1) // members
    for g in range(per_tile):
        lane_mask[g] = one(lane_group == g).astype(BF16)
    straight = one(down == across).astype(BF16)
    lapped = one((down + across == 0) | (down + across == count)).astype(BF16)
    flip = one(down + across == count - 1)
    sides = (((0,), (0,)), ((), ()))
    for copy in params:
        copy.wait()
    fdir[...] = lax.dot_general(filt[...], straight, sides, preferred_element_type=F32)
    frev[...] = lax.dot_general(filt[...], lapped, sides, preferred_element_type=F32)
    shortf[...] = short_in[...].astype(F32)

    def toeplitz(source, lhs, tile, near, far):
        for g in range(per_tile):
            row = tile * per_tile + g
            full = jnp.broadcast_to(source[row:row + 1, :], (STRIP, count))
            strip = pltpu.roll(full, 0, 1, stride=1, stride_axis=0).astype(BF16)
            for a in range(count // STRIP):
                ring = pltpu.roll(strip, a * STRIP, 1) if a else strip
                rows = slice(a * STRIP, (a + 1) * STRIP)
                at = slice(g * count + a * STRIP, g * count + (a + 1) * STRIP)
                lhs[tile, at, :count] = ring * near[rows]
                lhs[tile, at, count:] = ring * far[rows]

    def picked(product):
        total = product[:count]
        for g in range(1, per_tile):
            total = jnp.where(lane_group == g, product[g * count:(g + 1) * count], total)
        return total

    def lanes(tile):
        return pl.ds(tile * LANES, LANES)

    def span(c):
        return range(c * tiles, (c + 1) * tiles)

    for tile in span(0):
        toeplitz(frev, lhs_f, tile, m_own, m_prev)

    for c in range(chunks):
        @pl.when(before)
        def _():
            send_z(c).wait_recv()

        for tile in span(c):
            product = jnp.dot(lhs_f[tile], zz[:, lanes(tile)], preferred_element_type=F32)
            ysc[:, lanes(tile)] = picked(product)
            if c + 1 < chunks:
                toeplitz(frev, lhs_f, tile + tiles, m_own, m_prev)
            toeplitz(fdir, lhs_b, tile, t_own, t_next)
        hear(c)
        tell(c + 1)
    for r in range(chunks, len(reaches)):
        hear(r)
        tell(r + 1)

    def backward(c):
        @pl.when(after)
        def _():
            send_g(c).wait_recv()

        for tile in span(c):
            product = jnp.dot(lhs_b[tile], gg[:, lanes(tile)], preferred_element_type=F32)
            mixed = picked(product)
            key = qkv[1, :, lanes(tile)].astype(F32)
            value = qkv[2, :, lanes(tile)].astype(F32)
            dsc[1, pl.ds(0, count), lanes(tile)] = (mixed * value).astype(BF16).astype(F32)
            dsc[2, pl.ds(0, count), lanes(tile)] = (mixed * key).astype(BF16).astype(F32)

        @pl.when(before)
        def _():
            send_rim(c).start()

    def store(c):
        return pltpu.make_async_copy(
            obuf.at[:, :, cols(c)], out_hbm.at[0, :, :, cols(c)], out_sem.at[c])

    def short(c):
        @pl.when(after)
        def _():
            send_rim(c).wait_recv()

        def one_tile(i, carry):
            at = pl.ds(pl.multiple_of((c * tiles + i) * LANES, LANES), LANES)
            for s in range(3):
                total = dsc[s, pl.ds(0, count), at] * shortf[s, pl.ds(0, 1), at]
                for j in range(1, u_rows.shape[0] + 1):
                    moved = dsc[s, pl.ds(j, count), at]
                    weight = shortf[s, pl.ds(j, 1), at]
                    total = total + (moved * weight) * u_rows[j - 1]
                obuf[s, :, at] = total.astype(BF16)
            return carry

        lax.fori_loop(0, tiles, one_tile, 0)
        store(c).start()

    loads[0].wait()
    for c in range(chunks):
        send_inc(c).wait_recv()
        wide_inc = inc[:, cols(c)].astype(F32)
        own = (wide_inc * qkv[0, :, cols(c)].astype(F32)).astype(BF16)
        gg[pl.ds(0, count), cols(c)] = own

        @pl.when(before)
        def _():
            send_g(c).start()

        dsc[0, pl.ds(0, count), cols(c)] = (wide_inc * ysc[:, cols(c)]).astype(BF16).astype(F32)
        gback[:, cols(c)] = jnp.dot(
            flip.astype(BF16), own, preferred_element_type=F32).astype(BF16)
        for i, tile in enumerate(span(c)):
            back = gback[:, lanes(tile)]
            for g in range(per_tile):
                lhs_p[i, g * count:(g + 1) * count, :] = back * lane_mask[g]
            product = lax.dot_general(
                lhs_p[i], zz[:, lanes(tile)], (((1,), (1,)), ((), ())),
                preferred_element_type=F32)
            sums = []
            for g in range(per_tile):
                near = product[g * count:(g + 1) * count, :count]
                far = product[g * count:(g + 1) * count, count:]
                both = near * r_own[...] + far * r_prev[...]
                slid = pltpu.roll(both, 0, 1, stride=1, stride_axis=0)
                sums.append(jnp.sum(slid, axis=0, keepdims=True))
            acc[pl.ds(tile * per_tile, per_tile), :] = jnp.concatenate(sums, axis=0)

        if c == chunks - 1:
            for o in range(owners):
                part[o] = acc[o * share:(o + 1) * share, :]

            def start_part(o, carry):
                @pl.when(me != low + o)
                def _():
                    send_part(o).start()
                return carry

            lax.fori_loop(0, owners, start_part, 0)
        if c >= 1:
            backward(c - 1)
        if c >= 2:
            short(c - 2)

    backward(chunks - 1)
    owner = (me >= low) & (me < low + owners)

    @pl.when(owner)
    def _():
        def land_part(k, total):
            peer = lax.rem(me + k, devices)
            take_part(peer).wait_recv()
            return total + parts_in[peer]

        gath[me - low] = lax.fori_loop(1, devices, land_part, part[me - low])

        def start_sum(k, carry):
            send_sum(k).start()
            return carry

        lax.fori_loop(1, devices, start_sum, 0)

    for c in range(max(chunks - 2, 0), chunks):
        short(c)

    def land_sum(o, carry):
        @pl.when(me != low + o)
        def _():
            take_sum(o).wait_recv()
        return carry

    lax.fori_loop(0, owners, land_sum, 0)
    for o in range(owners):
        acc[o * share:(o + 1) * share, :] = gath[o]
    summed = lax.dot_general(
        flip, acc[...], (((1,), (1,)), ((), ())),
        preferred_element_type=F32, precision=lax.Precision.HIGHEST)
    fg[...] = summed / math.sqrt(count * devices * members)
    put = pltpu.make_async_copy(fg, sum_hbm.at[0], sum_sem)
    put.start()

    def left(o, carry):
        @pl.when(me != low + o)
        def _():
            send_part(o).wait_send()
        return carry

    lax.fori_loop(0, owners, left, 0)

    @pl.when(owner)
    def _():
        def left_sum(k, carry):
            send_sum(k).wait_send()
            return carry

        lax.fori_loop(1, devices, left_sum, 0)

    for c in range(chunks):
        send_inc(c).wait_send()
        store(c).wait()

        @pl.when(after)
        def _():
            send_z(c).wait_send()

        @pl.when(before)
        def _():
            send_g(c).wait_send()
            send_rim(c).wait_send()

    put.wait()


def put_out(grad_in, sums_in, grad_out, sums_out, sems):
    copies = [
        pltpu.make_async_copy(grad_in.at[0, i], grad_out.at[0, i], sems.at[i])
        for i in range(grad_in.shape[1])
    ]
    copies.append(pltpu.make_async_copy(sums_in, sums_out, sems.at[grad_in.shape[1]]))
    for copy in copies:
        copy.start()
    for copy in copies:
        copy.wait()


def body(sections, devices, saved_qkv, handed, long_filter, short_filter, doc_lengths):
    _, _, count, channels = saved_qkv.shape
    _, taps, groups = long_filter.shape
    short_taps = short_filter.shape[2]
    owners = max(1, devices // 2)
    assert taps == count and groups % owners == 0
    chunks = max(1, math.gcd(channels // LANES, 4))
    tiles = channels // LANES // chunks
    per_tile = LANES // (channels // groups)
    share = groups // owners
    dma = pltpu.SemaphoreType.DMA
    vmem = pltpu.VMEM
    hbm = pl.BlockSpec(memory_space=pl.ANY)
    saved_qkv, handed, long_filter, short_filter = [
        pltpu.with_memory_space_constraint(x, pltpu.HBM)
        for x in (saved_qkv, handed, long_filter, short_filter)
    ]
    grads, sums = pl.pallas_call(
        functools.partial(kernel, sections, devices, chunks, owners),
        out_shape=(
            pltpu.VMEM(saved_qkv.shape, BF16),
            pltpu.VMEM(long_filter.shape, F32),
        ),
        in_specs=[pl.BlockSpec(memory_space=pltpu.SMEM), hbm, hbm, hbm, hbm],
        out_specs=(hbm, hbm),
        scratch_shapes=[
            vmem((3, count, channels), BF16),
            vmem((count, channels), BF16),
            vmem((2 * count, channels), BF16),
            vmem((2 * count, channels), BF16),
            vmem((count, channels), BF16),
            vmem((count, channels), F32),
            vmem((3, count + RIM, channels), F32),
            vmem((3, count, channels), BF16),
            vmem((chunks * tiles, per_tile * count, 2 * count), BF16),
            vmem((chunks * tiles, per_tile * count, 2 * count), BF16),
            vmem((tiles, per_tile * count, LANES), BF16),
            vmem((groups, count), F32),
            vmem((groups, count), F32),
            vmem((count, groups), BF16),
            vmem((3, short_taps, channels), BF16),
            vmem((3, short_taps, channels), F32),
            vmem((count, count), BF16),
            vmem((count, count), BF16),
            vmem((count, count), BF16),
            vmem((count, count), BF16),
            vmem((count, count), F32),
            vmem((count, count), F32),
            vmem((short_taps - 1, count, LANES), F32),
            vmem((per_tile, count, LANES), BF16),
            vmem((groups, count), F32),
            vmem((owners, share, count), F32),
            vmem((devices, share, count), F32),
            vmem((owners, share, count), F32),
            vmem((count, groups), F32),
            dma((3,)), dma((2,)), dma((chunks,)), dma(()),
            dma((chunks,)), dma((chunks,)),
            dma((chunks,)), dma((chunks,)),
            dma((chunks,)), dma((chunks,)),
            dma((chunks,)), dma((chunks,)),
            dma((owners,)), dma((devices,)),
            dma((devices,)), dma((owners,)),
            pltpu.SemaphoreType.REGULAR((max(1, devices.bit_length()),)),
        ],
        compiler_params=pltpu.CompilerParams(
            collective_id=0, has_side_effects=True, vmem_limit_bytes=56 * 1024 * 1024),
    )(doc_lengths, saved_qkv, handed, long_filter, short_filter)
    return pl.pallas_call(
        put_out,
        out_shape=(
            jax.ShapeDtypeStruct(saved_qkv.shape, BF16),
            jax.ShapeDtypeStruct(long_filter.shape, F32),
        ),
        in_specs=[hbm, hbm],
        out_specs=(hbm, hbm),
        scratch_shapes=[dma((saved_qkv.shape[1] + 1,))],
        compiler_params=pltpu.CompilerParams(vmem_limit_bytes=1024 * 1024),
    )(grads, sums)


def solution(mesh):
    return jax.shard_map(
        functools.partial(body, mesh.shape["pipe"], mesh.shape["ctx"]),
        mesh=mesh,
        in_specs=(
            P("pipe", None, "ctx", None),
            P("pipe", "ctx", None),
            P("pipe", None, None),
            P("pipe", None, None, None),
            P(),
        ),
        out_specs=(P("pipe", None, "ctx", None), P("pipe", None, None)),
        check_vma=False,
    )
```

```python
import functools
import math

import jax
import jax.numpy as jnp
from jax import lax
from jax.experimental import pallas as pl
from jax.experimental.pallas import tpu as pltpu
from jax.sharding import PartitionSpec as P

MESH = pl.DeviceIdType.MESH
F32 = jnp.float32
BF16 = jnp.bfloat16
LANES = 128
RIM = 8
STRIP = 16


def positions(rows, docs_ref):
    latest = jnp.zeros(rows.shape, jnp.int32)
    start = jnp.int32(0)
    for doc in range(docs_ref.shape[0]):
        latest = jnp.maximum(latest, jnp.where(start <= rows, start, 0))
        start = start + docs_ref[doc]
    return rows - latest


def kernel(
    sections, devices, chunks, owners,
    docs_ref, qkv_hbm, handed_hbm, filt_hbm, short_hbm,
    out_hbm, sum_hbm,
    qkv, inc, zz, gg, gback, ysc, dsc, obuf, fdir, frev, filt, short_in, shortf,
    m_own, m_prev, t_own, t_next, r_own, r_prev, u_rows, lane_mask,
    acc, part_a, part_b, parts_in_a, parts_in_b, gath_a, gath_b, fg,
    in_sem, par_sem, out_sem, sum_sem, inc_s, inc_r, z_s, z_r, g_s, g_r, rim_s, rim_r, rs_s, rs_r, ag_s, ag_r,
    ready,
):
    sec = lax.axis_index("pipe")
    me = lax.axis_index("ctx")
    count, channels = inc.shape
    groups = fdir.shape[0]
    members = channels // groups
    per_tile = LANES // members
    wide = channels // chunks
    tiles = wide // LANES
    part, parts_in, gath = (part_a, part_b), (parts_in_a, parts_in_b), (gath_a, gath_b)
    low = (devices - owners) // 2
    first, last = me == 0, me == devices - 1
    ahead = lax.rem(sec + sections - 1, sections)
    behind = lax.rem(sec + 1, sections)
    before, after = jnp.logical_not(first), jnp.logical_not(last)

    barrier = pltpu.get_barrier_semaphore()
    pl.semaphore_signal(barrier, inc=1, device_id={"pipe": behind}, device_id_type=MESH)

    @pl.when(before)
    def _():
        pl.semaphore_signal(barrier, inc=1, device_id={"ctx": me - 1}, device_id_type=MESH)

    @pl.when(after)
    def _():
        pl.semaphore_signal(barrier, inc=1, device_id={"ctx": me + 1}, device_id_type=MESH)

    loads = [
        pltpu.make_async_copy(qkv_hbm.at[0, i], qkv.at[i], in_sem.at[i]) for i in range(3)
    ]
    for i in (1, 2, 0):
        loads[i].start()
    params = [
        pltpu.make_async_copy(filt_hbm.at[0], filt, par_sem.at[0]),
        pltpu.make_async_copy(short_hbm.at[0], short_in, par_sem.at[1]),
    ]
    for copy in params:
        copy.start()

    pl.semaphore_wait(barrier, 1 + before.astype(jnp.int32) + after.astype(jnp.int32))

    reaches = []
    while 2 ** len(reaches) < devices:
        reaches.append(2 ** len(reaches))

    def reach(r):
        return lax.shift_left(jnp.int32(1), jnp.int32(r))

    def tell(r):
        @pl.when((r < len(reaches)) & (me >= reach(r)))
        def _():
            pl.semaphore_signal(
                ready.at[r], inc=1, device_id={"ctx": me - reach(r)}, device_id_type=MESH)

        @pl.when((r < len(reaches)) & (me + reach(r) < devices))
        def _():
            pl.semaphore_signal(
                ready.at[r], inc=1, device_id={"ctx": me + reach(r)}, device_id_type=MESH)

    def hear(r):
        @pl.when(r < len(reaches))
        def _():
            pl.semaphore_wait(
                ready.at[r],
                (me >= reach(r)).astype(jnp.int32)
                + (me + reach(r) < devices).astype(jnp.int32))

    def cols(c):
        return pl.ds(pl.multiple_of(c * wide, wide), wide)

    def send_inc(c):
        return pltpu.make_async_remote_copy(
            handed_hbm.at[0, :, cols(c)], inc.at[:, cols(c)], inc_s.at[c], inc_r.at[c],
            device_id={"pipe": ahead}, device_id_type=MESH)

    def send_z(c):
        return pltpu.make_async_remote_copy(
            zz.at[pl.ds(0, count), cols(c)], zz.at[pl.ds(count, count), cols(c)],
            z_s.at[c], z_r.at[c],
            device_id={"ctx": lax.rem(me + 1, devices)}, device_id_type=MESH)

    def send_g(c):
        return pltpu.make_async_remote_copy(
            gg.at[pl.ds(0, count), cols(c)], gg.at[pl.ds(count, count), cols(c)],
            g_s.at[c], g_r.at[c],
            device_id={"ctx": lax.rem(me + devices - 1, devices)}, device_id_type=MESH)

    def send_rim(c):
        return pltpu.make_async_remote_copy(
            dsc.at[:, pl.ds(0, RIM), cols(c)], dsc.at[:, pl.ds(count, RIM), cols(c)],
            rim_s.at[c], rim_r.at[c],
            device_id={"ctx": lax.rem(me + devices - 1, devices)}, device_id_type=MESH)

    def send_part(b, o):
        return pltpu.make_async_remote_copy(
            part[b].at[o], parts_in[b].at[me], rs_s.at[b, o], rs_r.at[b, me],
            device_id={"ctx": low + o}, device_id_type=MESH)

    def take_part(b, peer):
        return pltpu.make_async_remote_copy(
            part[b].at[0], parts_in[b].at[peer], rs_s.at[b, 0], rs_r.at[b, peer],
            device_id={"ctx": peer}, device_id_type=MESH)

    def send_sum(b, k):
        return pltpu.make_async_remote_copy(
            gath[b].at[me - low], gath[b].at[me - low], ag_s.at[b, k], ag_r.at[b, me - low],
            device_id={"ctx": lax.rem(me + k, devices)}, device_id_type=MESH)

    def take_sum(b, o):
        return pltpu.make_async_remote_copy(
            gath[b].at[o], gath[b].at[o], ag_s.at[b, 0], ag_r.at[b, o],
            device_id={"ctx": low + o}, device_id_type=MESH)

    for c in range(chunks):
        send_inc(c).start()
    tell(0)

    loads[1].wait()
    loads[2].wait()
    for c in range(chunks):
        z = qkv[1, :, cols(c)].astype(F32) * qkv[2, :, cols(c)].astype(F32)
        zz[pl.ds(0, count), cols(c)] = z.astype(BF16)

        @pl.when(after)
        def _():
            send_z(c).start()

    @pl.when(first)
    def _():
        zz[pl.ds(count, count), :] = jnp.zeros((count, channels), BF16)

    @pl.when(last)
    def _():
        gg[pl.ds(count, count), :] = jnp.zeros((count, channels), BF16)
        dsc[:, pl.ds(count, RIM), :] = jnp.zeros((3, RIM, channels), F32)

    square = (count, count)
    down = lax.broadcasted_iota(jnp.int32, square, 0)
    across = lax.broadcasted_iota(jnp.int32, square, 1)
    base = me * count

    def one(flag):
        return jnp.where(flag, 1.0, 0.0).astype(F32)

    line = lax.broadcasted_iota(jnp.int32, (8, count), 1)

    def upright(rows):
        spread = jnp.broadcast_to(positions(rows, docs_ref)[0:1].astype(F32), square)
        return spread.T.astype(jnp.int32)

    pos_down = upright(base + line)
    lag = down - across
    m_own[...] = one((lag >= 0) & (lag <= pos_down)).astype(BF16)
    m_prev[...] = one((lag < 0) & (lag + count <= pos_down)).astype(BF16)
    turned = count - 1 - down
    pos_turned = upright(base + count - 1 - line)
    lag = turned - across
    r_own[...] = one((lag >= 0) & (lag <= pos_turned))
    r_prev[...] = one((lag < 0) & (lag + count <= pos_turned))
    pos_line = positions(base + line, docs_ref)[0:1]
    pos_ahead = positions(base + count + line, docs_ref)[0:1]
    lag = across - down
    t_own[...] = one((lag >= 0) & (lag <= pos_line)).astype(BF16)
    more = jnp.where(last, 0, 1)
    t_next[...] = one((lag < 0) & (lag + count <= pos_ahead) & (more > 0)).astype(BF16)
    for j in range(1, u_rows.shape[0] + 1):
        rows = base + down + j
        u_rows[j - 1] = one((j <= upright(base + line + j)) & (rows < devices * count))
    lane_group = lax.broadcasted_iota(jnp.int32, (count, LANES), 1) // members
    for g in range(per_tile):
        lane_mask[g] = one(lane_group == g).astype(BF16)
    straight = one(down == across).astype(BF16)
    lapped = one((down + across == 0) | (down + across == count)).astype(BF16)
    flip = one(down + across == count - 1)
    sides = (((0,), (0,)), ((), ()))
    for copy in params:
        copy.wait()
    fdir[...] = lax.dot_general(filt[...], straight, sides, preferred_element_type=F32)
    frev[...] = lax.dot_general(filt[...], lapped, sides, preferred_element_type=F32)
    shortf[...] = short_in[...].astype(F32)

    def applied(filters, near, far, tile, source):
        block = filters[pl.ds(pl.multiple_of(tile * per_tile, per_tile), per_tile), :]
        strips = []
        for g in range(per_tile):
            full = jnp.broadcast_to(block[g:g + 1], (STRIP, count))
            strip = pltpu.roll(full, 0, 1, stride=1, stride_axis=0).astype(BF16)
            for a in range(count // STRIP):
                ring = pltpu.roll(strip, a * STRIP, 1) if a else strip
                rows = slice(a * STRIP, (a + 1) * STRIP)
                strips.append(jnp.concatenate([ring * near[rows], ring * far[rows]], axis=1))
        product = jnp.dot(
            jnp.concatenate(strips, axis=0), source[:, lanes(tile)], preferred_element_type=F32)
        total = product[:count]
        for g in range(1, per_tile):
            total = jnp.where(lane_group == g, product[g * count:(g + 1) * count], total)
        return total

    def lanes(tile):
        return pl.ds(pl.multiple_of(tile * LANES, LANES), LANES)

    def forward(c, carry):
        @pl.when(before)
        def _():
            send_z(c).wait_recv()

        for i in range(tiles):
            tile = c * tiles + i
            ysc[:, lanes(tile)] = applied(frev, m_own, m_prev, tile, zz)
        hear(c)
        tell(c + 1)
        return carry

    lax.fori_loop(0, chunks, forward, 0)
    for r in range(chunks, len(reaches)):
        hear(r)
        tell(r + 1)

    def backward(c):
        @pl.when(after)
        def _():
            send_g(c).wait_recv()

        for i in range(tiles):
            tile = c * tiles + i
            mixed = applied(fdir, t_own, t_next, tile, gg)
            key = qkv[1, :, lanes(tile)].astype(F32)
            value = qkv[2, :, lanes(tile)].astype(F32)
            dsc[1, pl.ds(0, count), lanes(tile)] = (mixed * value).astype(BF16).astype(F32)
            dsc[2, pl.ds(0, count), lanes(tile)] = (mixed * key).astype(BF16).astype(F32)

        @pl.when(before)
        def _():
            send_rim(c).start()

    def store(c):
        return pltpu.make_async_copy(
            obuf.at[:, :, cols(c)], out_hbm.at[0, :, :, cols(c)], out_sem.at[c])

    def short(c):
        @pl.when(after)
        def _():
            send_rim(c).wait_recv()

        def one_tile(i, carry):
            at = pl.ds(pl.multiple_of((c * tiles + i) * LANES, LANES), LANES)
            for s in range(3):
                total = dsc[s, pl.ds(0, count), at] * shortf[s, pl.ds(0, 1), at]
                for j in range(1, u_rows.shape[0] + 1):
                    moved = dsc[s, pl.ds(j, count), at]
                    weight = shortf[s, pl.ds(j, 1), at]
                    total = total + (moved * weight) * u_rows[j - 1]
                obuf[s, :, at] = total.astype(BF16)
            return carry

        lax.fori_loop(0, tiles, one_tile, 0)
        store(c).start()

    def pairs(c):
        send_inc(c).wait_recv()
        wide_inc = inc[:, cols(c)].astype(F32)
        own = (wide_inc * qkv[0, :, cols(c)].astype(F32)).astype(BF16)
        gg[pl.ds(0, count), cols(c)] = own

        @pl.when(before)
        def _():
            send_g(c).start()

        dsc[0, pl.ds(0, count), cols(c)] = (wide_inc * ysc[:, cols(c)]).astype(BF16).astype(F32)
        gback[...] = jnp.dot(
            flip.astype(BF16), own, preferred_element_type=F32).astype(BF16)
        for i in range(tiles):
            tile = c * tiles + i
            back = gback[:, i * LANES:(i + 1) * LANES]
            spread = jnp.concatenate([back * lane_mask[g] for g in range(per_tile)], axis=0)
            product = lax.dot_general(
                spread, zz[:, lanes(tile)], (((1,), (1,)), ((), ())),
                preferred_element_type=F32)
            sums = []
            for g in range(per_tile):
                near = product[g * count:(g + 1) * count, :count]
                far = product[g * count:(g + 1) * count, count:]
                both = near * r_own[...] + far * r_prev[...]
                slid = pltpu.roll(both, 0, 1, stride=1, stride_axis=0)
                sums.append(jnp.sum(slid, axis=0, keepdims=True))
            acc[pl.ds(pl.multiple_of(tile * per_tile, per_tile), per_tile), :] = (
                jnp.concatenate(sums, axis=0))

    owner = (me >= low) & (me < low + owners)
    head = (chunks - 1) * (groups // chunks)
    batches = [(b, begin, part[b].shape[1]) for b, begin in ((0, 0), (1, head))]

    def scatter(b):
        _, begin, share = batches[b]
        for o in range(owners):
            part[b][o] = acc[begin + o * share:begin + (o + 1) * share, :]

        def start_part(o, carry):
            @pl.when(me != low + o)
            def _():
                send_part(b, o).start()
            return carry

        lax.fori_loop(0, owners, start_part, 0)

    def collect(b):
        def land_part(k, total):
            peer = lax.rem(me + k, devices)
            take_part(b, peer).wait_recv()
            return total + parts_in[b][peer]

        gath[b][me - low] = lax.fori_loop(1, devices, land_part, part[b][me - low])

        def start_sum(k, carry):
            send_sum(b, k).start()
            return carry

        lax.fori_loop(1, devices, start_sum, 0)

    loads[0].wait()

    def step(c, carry):
        @pl.when(c < chunks)
        def _():
            pairs(c)

        @pl.when(c == chunks - 2)
        def _():
            scatter(0)

        @pl.when(c == chunks - 1)
        def _():
            scatter(1)

        @pl.when((c >= 1) & (c <= chunks))
        def _():
            backward(c - 1)

        @pl.when((c == chunks - 1) & owner)
        def _():
            collect(0)

        @pl.when((c == chunks) & owner)
        def _():
            collect(1)

        @pl.when(c >= 2)
        def _():
            short(c - 2)

        return carry

    lax.fori_loop(0, chunks + 2, step, 0)

    for b, begin, share in batches:
        def land_sum(o, carry):
            @pl.when(me != low + o)
            def _():
                take_sum(b, o).wait_recv()
            return carry

        lax.fori_loop(0, owners, land_sum, 0)
        for o in range(owners):
            acc[begin + o * share:begin + (o + 1) * share, :] = gath[b][o]
    summed = lax.dot_general(
        flip, acc[...], (((1,), (1,)), ((), ())),
        preferred_element_type=F32, precision=lax.Precision.HIGHEST)
    fg[...] = summed / math.sqrt(count * devices * members)
    put = pltpu.make_async_copy(fg, sum_hbm.at[0], sum_sem)
    put.start()

    for b in range(2):
        def left(o, carry):
            @pl.when(me != low + o)
            def _():
                send_part(b, o).wait_send()
            return carry

        lax.fori_loop(0, owners, left, 0)

        @pl.when(owner)
        def _():
            def left_sum(k, carry):
                send_sum(b, k).wait_send()
                return carry

            lax.fori_loop(1, devices, left_sum, 0)

    for c in range(chunks):
        send_inc(c).wait_send()
        store(c).wait()

        @pl.when(after)
        def _():
            send_z(c).wait_send()

        @pl.when(before)
        def _():
            send_g(c).wait_send()
            send_rim(c).wait_send()

    put.wait()


def put_out(grad_in, sums_in, grad_out, sums_out, sems):
    copies = [
        pltpu.make_async_copy(grad_in.at[0, i], grad_out.at[0, i], sems.at[i])
        for i in range(grad_in.shape[1])
    ]
    copies.append(pltpu.make_async_copy(sums_in, sums_out, sems.at[grad_in.shape[1]]))
    for copy in copies:
        copy.start()
    for copy in copies:
        copy.wait()


def body(sections, devices, saved_qkv, handed, long_filter, short_filter, doc_lengths):
    _, _, count, channels = saved_qkv.shape
    _, taps, groups = long_filter.shape
    short_taps = short_filter.shape[2]
    owners = max(1, devices // 2)
    chunks = max(1, math.gcd(channels // LANES, 4))
    tiles = channels // LANES // chunks
    per_tile = LANES // (channels // groups)
    assert taps == count and chunks > 1 and groups % (owners * chunks) == 0
    shares = [rest * (groups // (owners * chunks)) for rest in (chunks - 1, 1)]
    dma = pltpu.SemaphoreType.DMA
    vmem = pltpu.VMEM
    hbm = pl.BlockSpec(memory_space=pl.ANY)
    saved_qkv, handed, long_filter, short_filter = [
        pltpu.with_memory_space_constraint(x, pltpu.HBM)
        for x in (saved_qkv, handed, long_filter, short_filter)
    ]
    grads, sums = pl.pallas_call(
        functools.partial(kernel, sections, devices, chunks, owners),
        out_shape=(
            pltpu.VMEM(saved_qkv.shape, BF16),
            pltpu.VMEM(long_filter.shape, F32),
        ),
        in_specs=[pl.BlockSpec(memory_space=pltpu.SMEM), hbm, hbm, hbm, hbm],
        out_specs=(hbm, hbm),
        scratch_shapes=[
            vmem((3, count, channels), BF16),
            vmem((count, channels), BF16),
            vmem((2 * count, channels), BF16),
            vmem((2 * count, channels), BF16),
            vmem((count, channels // chunks), BF16),
            vmem((count, channels), F32),
            vmem((3, count + RIM, channels), F32),
            vmem((3, count, channels), BF16),
            vmem((groups, count), F32),
            vmem((groups, count), F32),
            vmem((count, groups), BF16),
            vmem((3, short_taps, channels), BF16),
            vmem((3, short_taps, channels), F32),
            vmem((count, count), BF16),
            vmem((count, count), BF16),
            vmem((count, count), BF16),
            vmem((count, count), BF16),
            vmem((count, count), F32),
            vmem((count, count), F32),
            vmem((short_taps - 1, count, LANES), F32),
            vmem((per_tile, count, LANES), BF16),
            vmem((groups, count), F32),
            *[vmem((owners, share, count), F32) for share in shares],
            *[vmem((devices, share, count), F32) for share in shares],
            *[vmem((owners, share, count), F32) for share in shares],
            vmem((count, groups), F32),
            dma((3,)), dma((2,)), dma((chunks,)), dma(()),
            dma((chunks,)), dma((chunks,)),
            dma((chunks,)), dma((chunks,)),
            dma((chunks,)), dma((chunks,)),
            dma((chunks,)), dma((chunks,)),
            dma((2, owners)), dma((2, devices)),
            dma((2, devices)), dma((2, owners)),
            pltpu.SemaphoreType.REGULAR((max(1, devices.bit_length()),)),
        ],
        compiler_params=pltpu.CompilerParams(
            collective_id=0, has_side_effects=True, vmem_limit_bytes=56 * 1024 * 1024),
    )(doc_lengths, saved_qkv, handed, long_filter, short_filter)
    return pl.pallas_call(
        put_out,
        out_shape=(
            jax.ShapeDtypeStruct(saved_qkv.shape, BF16),
            jax.ShapeDtypeStruct(long_filter.shape, F32),
        ),
        in_specs=[hbm, hbm],
        out_specs=(hbm, hbm),
        scratch_shapes=[dma((saved_qkv.shape[1] + 1,))],
        compiler_params=pltpu.CompilerParams(vmem_limit_bytes=1024 * 1024),
    )(grads, sums)


def solution(mesh):
    return jax.shard_map(
        functools.partial(body, mesh.shape["pipe"], mesh.shape["ctx"]),
        mesh=mesh,
        in_specs=(
            P("pipe", None, "ctx", None),
            P("pipe", "ctx", None),
            P("pipe", None, None),
            P("pipe", None, None, None),
            P(),
        ),
        out_specs=(P("pipe", None, "ctx", None), P("pipe", None, None)),
        check_vma=False,
    )
```

```python
import functools
import math

import jax
import jax.numpy as jnp
from jax import lax
from jax.experimental import pallas as pl
from jax.experimental.pallas import tpu as pltpu
from jax.sharding import PartitionSpec as P

MESH = pl.DeviceIdType.MESH
F32 = jnp.float32
BF16 = jnp.bfloat16
LANES = 128
RIM = 8
STRIP = 16


def positions(rows, docs_ref):
    latest = jnp.zeros(rows.shape, jnp.int32)
    start = jnp.int32(0)
    for doc in range(docs_ref.shape[0]):
        latest = jnp.maximum(latest, jnp.where(start <= rows, start, 0))
        start = start + docs_ref[doc]
    return rows - latest


def kernel(
    sections, devices, chunks, owners,
    docs_ref, qkv_hbm, handed_hbm, filt_hbm, short_hbm,
    out_hbm, sum_hbm,
    qkv, inc, zz, gg, gback, dsc, obuf, fdir, frev, filt, short_in, shortf,
    m_own, m_prev, t_own, t_next, r_own, r_prev, u_rows, lane_mask,
    acc, part_a, part_b, parts_in_a, parts_in_b, gath_a, gath_b, fg,
    in_sem, par_sem, out_sem, sum_sem, inc_s, inc_r, z_s, z_r, g_s, g_r, rim_s, rim_r, rs_s, rs_r, ag_s, ag_r,
    ready,
):
    sec = lax.axis_index("pipe")
    me = lax.axis_index("ctx")
    count, channels = inc.shape
    groups = fdir.shape[0]
    members = channels // groups
    per_tile = LANES // members
    wide = channels // chunks
    tiles = wide // LANES
    part, parts_in, gath = (part_a, part_b), (parts_in_a, parts_in_b), (gath_a, gath_b)
    low = (devices - owners) // 2
    first, last = me == 0, me == devices - 1
    ahead = lax.rem(sec + sections - 1, sections)
    behind = lax.rem(sec + 1, sections)
    before, after = jnp.logical_not(first), jnp.logical_not(last)

    barrier = pltpu.get_barrier_semaphore()
    pl.semaphore_signal(barrier, inc=1, device_id={"pipe": behind}, device_id_type=MESH)

    @pl.when(before)
    def _():
        pl.semaphore_signal(barrier, inc=1, device_id={"ctx": me - 1}, device_id_type=MESH)

    @pl.when(after)
    def _():
        pl.semaphore_signal(barrier, inc=1, device_id={"ctx": me + 1}, device_id_type=MESH)

    loads = [
        pltpu.make_async_copy(qkv_hbm.at[0, i], qkv.at[i], in_sem.at[i]) for i in range(3)
    ]
    for i in (1, 2, 0):
        loads[i].start()
    params = [
        pltpu.make_async_copy(filt_hbm.at[0], filt, par_sem.at[0]),
        pltpu.make_async_copy(short_hbm.at[0], short_in, par_sem.at[1]),
    ]
    for copy in params:
        copy.start()

    pl.semaphore_wait(barrier, 1 + before.astype(jnp.int32) + after.astype(jnp.int32))

    reaches = []
    while 2 ** len(reaches) < devices:
        reaches.append(2 ** len(reaches))

    def reach(r):
        return lax.shift_left(jnp.int32(1), jnp.int32(r))

    def tell(r):
        @pl.when((r < len(reaches)) & (me >= reach(r)))
        def _():
            pl.semaphore_signal(
                ready.at[r], inc=1, device_id={"ctx": me - reach(r)}, device_id_type=MESH)

        @pl.when((r < len(reaches)) & (me + reach(r) < devices))
        def _():
            pl.semaphore_signal(
                ready.at[r], inc=1, device_id={"ctx": me + reach(r)}, device_id_type=MESH)

    def hear(r):
        @pl.when(r < len(reaches))
        def _():
            pl.semaphore_wait(
                ready.at[r],
                (me >= reach(r)).astype(jnp.int32)
                + (me + reach(r) < devices).astype(jnp.int32))

    def cols(c):
        return pl.ds(pl.multiple_of(c * wide, wide), wide)

    def send_inc(c):
        return pltpu.make_async_remote_copy(
            handed_hbm.at[0, :, cols(c)], inc.at[:, cols(c)], inc_s.at[c], inc_r.at[c],
            device_id={"pipe": ahead}, device_id_type=MESH)

    def send_z(c):
        return pltpu.make_async_remote_copy(
            zz.at[pl.ds(0, count), cols(c)], zz.at[pl.ds(count, count), cols(c)],
            z_s.at[c], z_r.at[c],
            device_id={"ctx": lax.rem(me + 1, devices)}, device_id_type=MESH)

    def send_g(c):
        return pltpu.make_async_remote_copy(
            gg.at[pl.ds(0, count), cols(c)], gg.at[pl.ds(count, count), cols(c)],
            g_s.at[c], g_r.at[c],
            device_id={"ctx": lax.rem(me + devices - 1, devices)}, device_id_type=MESH)

    def send_rim(c):
        return pltpu.make_async_remote_copy(
            dsc.at[:, pl.ds(0, RIM), cols(c)], dsc.at[:, pl.ds(count, RIM), cols(c)],
            rim_s.at[c], rim_r.at[c],
            device_id={"ctx": lax.rem(me + devices - 1, devices)}, device_id_type=MESH)

    def send_part(b, o):
        return pltpu.make_async_remote_copy(
            part[b].at[o], parts_in[b].at[me], rs_s.at[b, o], rs_r.at[b, me],
            device_id={"ctx": low + o}, device_id_type=MESH)

    def take_part(b, peer):
        return pltpu.make_async_remote_copy(
            part[b].at[0], parts_in[b].at[peer], rs_s.at[b, 0], rs_r.at[b, peer],
            device_id={"ctx": peer}, device_id_type=MESH)

    def send_sum(b, k):
        return pltpu.make_async_remote_copy(
            gath[b].at[me - low], gath[b].at[me - low], ag_s.at[b, k], ag_r.at[b, me - low],
            device_id={"ctx": lax.rem(me + k, devices)}, device_id_type=MESH)

    def take_sum(b, o):
        return pltpu.make_async_remote_copy(
            gath[b].at[o], gath[b].at[o], ag_s.at[b, 0], ag_r.at[b, o],
            device_id={"ctx": low + o}, device_id_type=MESH)

    for c in range(chunks):
        send_inc(c).start()
    tell(0)

    loads[1].wait()
    loads[2].wait()
    for c in range(chunks):
        z = qkv[1, :, cols(c)].astype(F32) * qkv[2, :, cols(c)].astype(F32)
        zz[pl.ds(0, count), cols(c)] = z.astype(BF16)

        @pl.when(after)
        def _():
            send_z(c).start()

    hear(0)
    tell(1)

    @pl.when(first)
    def _():
        zz[pl.ds(count, count), :] = jnp.zeros((count, channels), BF16)

    @pl.when(last)
    def _():
        gg[pl.ds(count, count), :] = jnp.zeros((count, channels), BF16)
        dsc[:, pl.ds(count, RIM), :] = jnp.zeros((3, RIM, channels), F32)

    square = (count, count)
    down = lax.broadcasted_iota(jnp.int32, square, 0)
    across = lax.broadcasted_iota(jnp.int32, square, 1)
    base = me * count

    def one(flag):
        return jnp.where(flag, 1.0, 0.0).astype(F32)

    line = lax.broadcasted_iota(jnp.int32, (8, count), 1)

    def upright(rows):
        spread = jnp.broadcast_to(positions(rows, docs_ref)[0:1].astype(F32), square)
        return spread.T.astype(jnp.int32)

    pos_down = upright(base + line)
    lag = down - across
    m_own[...] = one((lag >= 0) & (lag <= pos_down)).astype(BF16)
    m_prev[...] = one((lag < 0) & (lag + count <= pos_down)).astype(BF16)
    turned = count - 1 - down
    pos_turned = upright(base + count - 1 - line)
    lag = turned - across
    r_own[...] = one((lag >= 0) & (lag <= pos_turned))
    r_prev[...] = one((lag < 0) & (lag + count <= pos_turned))
    pos_line = positions(base + line, docs_ref)[0:1]
    pos_ahead = positions(base + count + line, docs_ref)[0:1]
    lag = across - down
    t_own[...] = one((lag >= 0) & (lag <= pos_line)).astype(BF16)
    more = jnp.where(last, 0, 1)
    t_next[...] = one((lag < 0) & (lag + count <= pos_ahead) & (more > 0)).astype(BF16)
    for j in range(1, u_rows.shape[0] + 1):
        rows = base + down + j
        u_rows[j - 1] = one((j <= upright(base + line + j)) & (rows < devices * count))
    lane_group = lax.broadcasted_iota(jnp.int32, (count, LANES), 1) // members
    for g in range(per_tile):
        lane_mask[g] = one(lane_group == g).astype(BF16)
    straight = one(down == across).astype(BF16)
    lapped = one((down + across == 0) | (down + across == count)).astype(BF16)
    flip = one(down + across == count - 1)
    sides = (((0,), (0,)), ((), ()))
    for copy in params:
        copy.wait()
    fdir[...] = lax.dot_general(filt[...], straight, sides, preferred_element_type=F32)
    frev[...] = lax.dot_general(filt[...], lapped, sides, preferred_element_type=F32)
    shortf[...] = short_in[...].astype(F32)

    hear(1)
    tell(2)

    def applied(filters, near, far, tile, source):
        block = filters[pl.ds(pl.multiple_of(tile * per_tile, per_tile), per_tile), :]
        strips = []
        for g in range(per_tile):
            full = jnp.broadcast_to(block[g:g + 1], (STRIP, count))
            strip = pltpu.roll(full, 0, 1, stride=1, stride_axis=0).astype(BF16)
            for a in range(count // STRIP):
                ring = pltpu.roll(strip, a * STRIP, 1) if a else strip
                rows = slice(a * STRIP, (a + 1) * STRIP)
                strips.append(jnp.concatenate([ring * near[rows], ring * far[rows]], axis=1))
        product = jnp.dot(
            jnp.concatenate(strips, axis=0), source[:, lanes(tile)], preferred_element_type=F32)
        total = product[:count]
        for g in range(1, per_tile):
            total = jnp.where(lane_group == g, product[g * count:(g + 1) * count], total)
        return total

    def lanes(tile):
        return pl.ds(pl.multiple_of(tile * LANES, LANES), LANES)

    rounds = pl.cdiv(max(len(reaches) - 2, 1), chunks - 2)

    def forward(c):
        for i in range(tiles):
            at = lanes(c * tiles + i)
            total = applied(frev, m_own, m_prev, c * tiles + i, zz)
            dsc[0, pl.ds(0, count), at] = (
                inc[:, at].astype(F32) * total).astype(BF16).astype(F32)

    def backward(c):
        @pl.when(after)
        def _():
            send_g(c).wait_recv()

        for i in range(tiles):
            tile = c * tiles + i
            mixed = applied(fdir, t_own, t_next, tile, gg)
            key = qkv[1, :, lanes(tile)].astype(F32)
            value = qkv[2, :, lanes(tile)].astype(F32)
            dsc[1, pl.ds(0, count), lanes(tile)] = (mixed * value).astype(BF16).astype(F32)
            dsc[2, pl.ds(0, count), lanes(tile)] = (mixed * key).astype(BF16).astype(F32)

        @pl.when(before)
        def _():
            send_rim(c).start()

    def store(c):
        return pltpu.make_async_copy(
            obuf.at[:, :, cols(c)], out_hbm.at[0, :, :, cols(c)], out_sem.at[c])

    def short(c):
        @pl.when(after)
        def _():
            send_rim(c).wait_recv()

        def one_tile(i, carry):
            at = pl.ds(pl.multiple_of((c * tiles + i) * LANES, LANES), LANES)
            for s in range(3):
                total = dsc[s, pl.ds(0, count), at] * shortf[s, pl.ds(0, 1), at]
                for j in range(1, u_rows.shape[0] + 1):
                    moved = dsc[s, pl.ds(j, count), at]
                    weight = shortf[s, pl.ds(j, 1), at]
                    total = total + (moved * weight) * u_rows[j - 1]
                obuf[s, :, at] = total.astype(BF16)
            return carry

        lax.fori_loop(0, tiles, one_tile, 0)
        store(c).start()

    def pairs(c):
        send_inc(c).wait_recv()
        wide_inc = inc[:, cols(c)].astype(F32)
        own = (wide_inc * qkv[0, :, cols(c)].astype(F32)).astype(BF16)
        gg[pl.ds(0, count), cols(c)] = own

        @pl.when(before)
        def _():
            send_g(c).start()

        @pl.when(before)
        def _():
            send_z(c).wait_recv()

        gback[...] = jnp.dot(
            flip.astype(BF16), own, preferred_element_type=F32).astype(BF16)
        for i in range(tiles):
            tile = c * tiles + i
            back = gback[:, i * LANES:(i + 1) * LANES]
            spread = jnp.concatenate([back * lane_mask[g] for g in range(per_tile)], axis=0)
            product = lax.dot_general(
                spread, zz[:, lanes(tile)], (((1,), (1,)), ((), ())),
                preferred_element_type=F32)
            sums = []
            for g in range(per_tile):
                near = product[g * count:(g + 1) * count, :count]
                far = product[g * count:(g + 1) * count, count:]
                both = near * r_own[...] + far * r_prev[...]
                slid = pltpu.roll(both, 0, 1, stride=1, stride_axis=0)
                sums.append(jnp.sum(slid, axis=0, keepdims=True))
            acc[pl.ds(pl.multiple_of(tile * per_tile, per_tile), per_tile), :] = (
                jnp.concatenate(sums, axis=0))

    owner = (me >= low) & (me < low + owners)
    head = (chunks - 1) * (groups // chunks)
    batches = [(b, begin, part[b].shape[1]) for b, begin in ((0, 0), (1, head))]

    def scatter(b):
        _, begin, share = batches[b]
        for o in range(owners):
            part[b][o] = acc[begin + o * share:begin + (o + 1) * share, :]

        def start_part(o, carry):
            @pl.when(me != low + o)
            def _():
                send_part(b, o).start()
            return carry

        lax.fori_loop(0, owners, start_part, 0)

    def collect(b):
        def land_part(k, total):
            peer = lax.rem(me + k, devices)
            take_part(b, peer).wait_recv()
            return total + parts_in[b][peer]

        gath[b][me - low] = lax.fori_loop(1, devices, land_part, part[b][me - low])

        def start_sum(k, carry):
            send_sum(b, k).start()
            return carry

        lax.fori_loop(1, devices, start_sum, 0)

    loads[0].wait()

    def step(c, carry):
        @pl.when(c < chunks)
        def _():
            pairs(c)

        @pl.when(c == chunks - 2)
        def _():
            scatter(0)

        @pl.when(c == chunks - 1)
        def _():
            scatter(1)

        @pl.when(c < chunks)
        def _():
            forward(c)

        @pl.when(c < chunks - 2)
        def _():
            for q in range(rounds):
                hear(c * rounds + q + 2)
                tell(c * rounds + q + 3)

        @pl.when((c >= 1) & (c <= chunks))
        def _():
            backward(c - 1)

        @pl.when((c == chunks - 1) & owner)
        def _():
            collect(0)

        @pl.when((c == chunks) & owner)
        def _():
            collect(1)

        @pl.when(c >= 2)
        def _():
            short(c - 2)

        return carry

    lax.fori_loop(0, chunks + 2, step, 0)

    for b, begin, share in batches:
        def land_sum(o, carry):
            @pl.when(me != low + o)
            def _():
                take_sum(b, o).wait_recv()
            return carry

        lax.fori_loop(0, owners, land_sum, 0)
        for o in range(owners):
            acc[begin + o * share:begin + (o + 1) * share, :] = gath[b][o]
    summed = lax.dot_general(
        flip, acc[...], (((1,), (1,)), ((), ())),
        preferred_element_type=F32, precision=lax.Precision.HIGHEST)
    fg[...] = summed / math.sqrt(count * devices * members)
    put = pltpu.make_async_copy(fg, sum_hbm.at[0], sum_sem)
    put.start()

    for b in range(2):
        def left(o, carry):
            @pl.when(me != low + o)
            def _():
                send_part(b, o).wait_send()
            return carry

        lax.fori_loop(0, owners, left, 0)

        @pl.when(owner)
        def _():
            def left_sum(k, carry):
                send_sum(b, k).wait_send()
                return carry

            lax.fori_loop(1, devices, left_sum, 0)

    for c in range(chunks):
        send_inc(c).wait_send()
        store(c).wait()

        @pl.when(after)
        def _():
            send_z(c).wait_send()

        @pl.when(before)
        def _():
            send_g(c).wait_send()
            send_rim(c).wait_send()

    put.wait()


def put_out(grad_in, sums_in, grad_out, sums_out, sems):
    copies = [
        pltpu.make_async_copy(grad_in.at[0, i], grad_out.at[0, i], sems.at[i])
        for i in range(grad_in.shape[1])
    ]
    copies.append(pltpu.make_async_copy(sums_in, sums_out, sems.at[grad_in.shape[1]]))
    for copy in copies:
        copy.start()
    for copy in copies:
        copy.wait()


def body(sections, devices, saved_qkv, handed, long_filter, short_filter, doc_lengths):
    _, _, count, channels = saved_qkv.shape
    _, taps, groups = long_filter.shape
    short_taps = short_filter.shape[2]
    owners = max(1, devices // 2)
    chunks = max(1, math.gcd(channels // LANES, 4))
    tiles = channels // LANES // chunks
    per_tile = LANES // (channels // groups)
    assert taps == count and chunks > 2 and groups % (owners * chunks) == 0
    shares = [rest * (groups // (owners * chunks)) for rest in (chunks - 1, 1)]
    dma = pltpu.SemaphoreType.DMA
    vmem = pltpu.VMEM
    hbm = pl.BlockSpec(memory_space=pl.ANY)
    saved_qkv, handed, long_filter, short_filter = [
        pltpu.with_memory_space_constraint(x, pltpu.HBM)
        for x in (saved_qkv, handed, long_filter, short_filter)
    ]
    grads, sums = pl.pallas_call(
        functools.partial(kernel, sections, devices, chunks, owners),
        out_shape=(
            pltpu.VMEM(saved_qkv.shape, BF16),
            pltpu.VMEM(long_filter.shape, F32),
        ),
        in_specs=[pl.BlockSpec(memory_space=pltpu.SMEM), hbm, hbm, hbm, hbm],
        out_specs=(hbm, hbm),
        scratch_shapes=[
            vmem((3, count, channels), BF16),
            vmem((count, channels), BF16),
            vmem((2 * count, channels), BF16),
            vmem((2 * count, channels), BF16),
            vmem((count, channels // chunks), BF16),
            vmem((3, count + RIM, channels), F32),
            vmem((3, count, channels), BF16),
            vmem((groups, count), F32),
            vmem((groups, count), F32),
            vmem((count, groups), BF16),
            vmem((3, short_taps, channels), BF16),
            vmem((3, short_taps, channels), F32),
            vmem((count, count), BF16),
            vmem((count, count), BF16),
            vmem((count, count), BF16),
            vmem((count, count), BF16),
            vmem((count, count), F32),
            vmem((count, count), F32),
            vmem((short_taps - 1, count, LANES), F32),
            vmem((per_tile, count, LANES), BF16),
            vmem((groups, count), F32),
            *[vmem((owners, share, count), F32) for share in shares],
            *[vmem((devices, share, count), F32) for share in shares],
            *[vmem((owners, share, count), F32) for share in shares],
            vmem((count, groups), F32),
            dma((3,)), dma((2,)), dma((chunks,)), dma(()),
            dma((chunks,)), dma((chunks,)),
            dma((chunks,)), dma((chunks,)),
            dma((chunks,)), dma((chunks,)),
            dma((chunks,)), dma((chunks,)),
            dma((2, owners)), dma((2, devices)),
            dma((2, devices)), dma((2, owners)),
            pltpu.SemaphoreType.REGULAR((max(1, devices.bit_length()),)),
        ],
        compiler_params=pltpu.CompilerParams(
            collective_id=0, has_side_effects=True, vmem_limit_bytes=56 * 1024 * 1024),
    )(doc_lengths, saved_qkv, handed, long_filter, short_filter)
    return pl.pallas_call(
        put_out,
        out_shape=(
            jax.ShapeDtypeStruct(saved_qkv.shape, BF16),
            jax.ShapeDtypeStruct(long_filter.shape, F32),
        ),
        in_specs=[hbm, hbm],
        out_specs=(hbm, hbm),
        scratch_shapes=[dma((saved_qkv.shape[1] + 1,))],
        compiler_params=pltpu.CompilerParams(vmem_limit_bytes=1024 * 1024),
    )(grads, sums)


def solution(mesh):
    return jax.shard_map(
        functools.partial(body, mesh.shape["pipe"], mesh.shape["ctx"]),
        mesh=mesh,
        in_specs=(
            P("pipe", None, "ctx", None),
            P("pipe", "ctx", None),
            P("pipe", None, None),
            P("pipe", None, None, None),
            P(),
        ),
        out_specs=(P("pipe", None, "ctx", None), P("pipe", None, None)),
        check_vma=False,
    )
```
